32 devices in a mesh: dp: 2 (over y), expert: 4 (over z), tile: 4 (over x, core).
Axes of the slice: x: 2, y: 2, z: 4, core: 2. Of those that a mesh axis runs over, the one named last changes fastest.
Arguments:
- tokens: bfloat16 [512, 4096], P(('dp', 'expert'), 'tile'), may hold values from -6 to 6
- hidden: bfloat16 [512, 2, 7168], P(('dp', 'expert'), None, 'tile'), may hold values from -6 to 6
- routes: int32 [512, 2], P(('dp', 'expert')), may hold values from 0 to 3, all different within a row; in each aligned block of 64 rows (0 to 63, 64 to 127, ...) at most 40 rows name the same one
- lengths: int32 [8], P(('dp', 'expert')), may hold values from 1 to 64, as said below
Outputs:
- hessian_in: float32 [4, 4096, 4096], P('expert', 'tile', 'dp')
- hessian_down: float32 [4, 7168, 7168], P('expert', 'tile', 'dp')
The draws below stay inside these ranges and needn't reach their ends.
Inputs may be any that keep to these rules, and one draw needn't show every extreme that they name: `routes`: in each aligned block of 64 rows (the rows of one group) no expert is named by more than 40 rows, a bound that some block reaches. The live rows of group g are its first lengths[g] rows; the last group is full.
All inputs are finite; a program needn't handle non-finite values.
Results may differ from the reference program's by a relative error of at most 0.0003.
Values may be sent and summed in bfloat16 or wider, within the bound.
A program may use at most 128 MiB of HBM per device.

```python
import math
import jax
import jax.numpy as jnp
import numpy as np
from jax import lax

D = 4096
FFW = 7168
TOP = 2
TOK_DEV = 64
EXPERTS = 4
GROUPS = 8
TOKENS = 512
CAP = 40


def draw_lengths(key, part):
    group_index = jnp.arange(GROUPS, dtype=jnp.int32)
    lowest = TOK_DEV // 3
    rising = lowest + (TOK_DEV - lowest) * group_index // max(GROUPS - 1, 1)
    jitter = jax.random.randint(key, (GROUPS,), 0, max(TOK_DEV // 8, 1), dtype=jnp.int32)
    jitter = jnp.where(group_index == GROUPS - 1, 0, jitter)
    return jnp.maximum(rising - jitter, 1).astype(jnp.int32)


def steps_of(stream_key, dims, shards, low, top_value):
    gain = 1.0
    for axis_at, parts in shards:
        heights = jax.random.uniform(jax.random.fold_in(jax.random.fold_in(stream_key, 6), axis_at), (parts,), jnp.float32, low / len(shards), top_value / len(shards))
        gain = gain * jnp.repeat(jnp.exp(heights), dims[axis_at] // parts).reshape((-1,) + (1,) * (len(dims) - 1 - axis_at))
    return gain


def assign_block(own_key, own, number, rows, number_of, top, bound, slope):
    order = jax.random.permutation(own_key, number_of)
    crowded, ordinary = portions_of(number_of, rows * top, bound, slope, True), portions_of(number_of, rows * top, bound, slope, False)
    places = jnp.arange(number_of)

    def named(sizes, rotation):
        used = int((sizes > 0).sum())
        fixed = max(1, used // 4)
        passed = fixed + (places - fixed + rotation * (used - fixed)) % max(1, number_of - fixed)
        return jnp.zeros((number_of,), jnp.int32).at[order[jnp.where(places < fixed, places, passed)]].set(jnp.asarray(sizes, jnp.int32))

    sizes = jnp.where(number % 4 == 0, named(crowded, number // 4), named(ordinary, number - number // 4 - 1))
    mixed = jax.random.permutation(jax.random.fold_in(own, 3), number_of)
    source_of, receiver = mixed[0:number_of // 2 * 2:2], mixed[1:number_of // 2 * 2:2]
    room = jnp.minimum(sizes[source_of] - 1, bound - sizes[receiver]) // 2
    room = jnp.where((source_of == order[0]) | (receiver == order[0]) | (sizes[receiver] == 0), 0, jnp.maximum(room, 0))
    passed = jax.random.randint(jax.random.fold_in(own, 4), (number_of // 2,), 0, 1 << 20) % (room + 1)
    sizes = sizes.at[source_of].add(-passed).at[receiver].add(passed)
    members = jnp.searchsorted(jnp.cumsum(sizes), jnp.arange(rows * top), side="right").astype(jnp.int32)
    grid = members.reshape(top, rows).T
    grid = grid[jax.random.permutation(jax.random.fold_in(own, 1), rows)]
    rotation = jax.random.randint(jax.random.fold_in(own, 2), (rows, 1), 0, top)
    return jnp.take_along_axis(grid, (jnp.arange(top)[None, :] + rotation) % top, axis=1)


def portions_of(count, total, limit, slope, full):
    loads = [(1 << 20) // math.isqrt(rank ** slope) + 1 for rank in range(1, count + 1)]
    largest = limit if full else min(limit, max(-(-total // count), total * loads[0] // sum(loads)))
    least = 1 if total - largest >= count - 1 else 0
    counts, spare = [largest] + [least] * (count - 1), total - largest - least * (count - 1)
    while spare > 0:
        candidates = [i for i in range(1, count) if counts[i] < largest] or [i for i in range(1, count) if counts[i] < limit]
        pool, budget = sum([loads[i] for i in candidates]), spare
        for i in candidates:
            addition = min(limit - counts[i], max(1, budget * loads[i] // pool), spare)
            counts[i] = counts[i] + addition
            spare = spare - addition
    return np.array(counts)


def gaussian(key, shape, spread, reach, pieces=(), kind=jnp.bfloat16):
    drawn = jax.random.normal(key, shape, jnp.float32) * spread
    if len(pieces) > 0:
        drawn = steps_of(key, shape, pieces, -0.22, 0.18) * drawn
    return jnp.clip(drawn, min=-reach, max=reach).astype(kind)


def setup_inputs(seed: int = 0) -> dict:
    streams_of = jax.random.split(jax.random.key(seed), 5)
    tokens = gaussian(streams_of[0], (TOKENS, D), 1.0, 6.0, ((0, 8), (1, 4)))
    hidden = gaussian(streams_of[1], (TOKENS, TOP, FFW), 1.0, 6.0, ((0, 8), (2, 4)))
    routes_keys = jax.random.split(jax.random.fold_in(streams_of[2], 1), TOKENS // TOK_DEV)
    routes_turns = jax.random.permutation(jax.random.fold_in(streams_of[2], 3), TOKENS // TOK_DEV)
    routes = jax.vmap(lambda own, number: assign_block(jax.random.fold_in(streams_of[2], 2), own, number, TOK_DEV, EXPERTS, TOP, CAP, 1))(routes_keys, routes_turns).reshape((TOKENS, TOP))
    lengths = draw_lengths(jax.random.fold_in(streams_of[4], 71), 0)
    return dict(tokens=tokens, hidden=hidden, routes=routes, lengths=lengths)


def reference(tokens, hidden, routes, lengths):
    token_total = tokens.shape[0]
    token_index = jnp.arange(token_total, dtype=jnp.int32)
    live_mask = (token_index % TOK_DEV) < lengths[token_index // TOK_DEV]
    row_limit = GROUPS * CAP

    def one_expert(expert):
        picked = (routes == expert) & live_mask[:, None]
        token_hit = jnp.any(picked, axis=1)
        pair_count = jnp.sum(picked.astype(jnp.float32))
        ordering = jnp.argsort(jnp.where(token_hit, 0, 1).astype(jnp.int32), stable=True)[:row_limit]
        chosen = tokens[ordering] * token_hit[ordering][:, None].astype(jnp.bfloat16)
        weights = picked[ordering].astype(jnp.float32)
        chosen_hidden = jnp.sum(hidden[ordering].astype(jnp.float32) * weights[:, :, None], axis=1).astype(jnp.bfloat16)
        factor = jnp.float32(2.0) / jnp.maximum(pair_count, jnp.float32(1.0))
        gram_tokens = jnp.dot(chosen.T, chosen, preferred_element_type=jnp.float32) * factor
        gram_hidden = jnp.dot(chosen_hidden.T, chosen_hidden, preferred_element_type=jnp.float32) * factor
        return gram_tokens, gram_hidden

    hessian_in, hessian_down = lax.map(one_expert, jnp.arange(EXPERTS, dtype=jnp.int32))
    return hessian_in, hessian_down
```

```python
import functools

import jax
import jax.numpy as jnp
from jax import lax
from jax.experimental import pallas as pl
from jax.experimental.pallas import tpu as pltpu
from jax.sharding import PartitionSpec as P

MESH = pl.DeviceIdType.MESH
ROW_BLOCK = 256


def broadcast(value, axis, source):
    kept = jnp.where(lax.axis_index(axis) == source, value, 0).astype(value.dtype)
    return lax.psum(kept, axis)


def contract(left, right):
    return lax.dot_general(
        left, right, (((0,), (0,)), ((), ())), preferred_element_type=jnp.float32
    )


def dispatch_tables(routes, live_count, experts, share_size, senders):
    token_count = routes.shape[0]
    top_count = routes.shape[1]
    flat_routes = routes.reshape(token_count * top_count)
    pair_index = jnp.arange(token_count * top_count, dtype=jnp.int32)
    pair_live = pair_index // top_count < live_count
    expert_ids = jnp.arange(experts, dtype=jnp.int32)
    onehot = ((flat_routes[:, None] == expert_ids[None, :]) & pair_live[:, None]).astype(
        jnp.float32
    )
    before = jnp.cumsum(onehot, axis=0) - onehot
    position = jnp.sum(before * onehot, axis=1).astype(jnp.int32)
    target = (
        position // share_size * (experts * share_size)
        + flat_routes * share_size
        + position % share_size
    )
    slot_total = senders * experts * share_size
    placed = (target[None, :] == jnp.arange(slot_total, dtype=jnp.int32)[:, None]) & pair_live[
        None, :
    ]
    return (placed.astype(jnp.float32), jnp.sum(onehot, axis=0))


def general(tokens, hidden, routes, lengths):
    experts = lax.axis_size("expert")
    senders = lax.axis_size("dp")
    tiles = lax.axis_size("tile")
    token_count = tokens.shape[0]
    top_count = routes.shape[1]
    share_size = (5 * token_count + 2 * experts * senders - 1) // (2 * experts * senders)
    placed, local_counts = dispatch_tables(routes, lengths[0], experts, share_size, senders)
    slot_total = placed.shape[0]
    by_token = jnp.sum(placed.reshape(slot_total, token_count, top_count), axis=2).astype(
        jnp.bfloat16
    )
    send_tokens = jnp.dot(by_token, tokens, preferred_element_type=jnp.float32).astype(jnp.bfloat16)
    flat_hidden = hidden.reshape(token_count * top_count, hidden.shape[2])
    send_hidden = jnp.dot(
        placed.astype(jnp.bfloat16), flat_hidden, preferred_element_type=jnp.float32
    ).astype(jnp.bfloat16)
    slot_tokens, slot_hidden = (
        lax.all_to_all(send_tokens, ("dp", "expert"), split_axis=0, concat_axis=0, tiled=True),
        lax.all_to_all(send_hidden, ("dp", "expert"), split_axis=0, concat_axis=0, tiled=True),
    )
    global_counts = lax.psum(local_counts, ("dp", "expert"))
    own_expert = lax.axis_index("expert")
    own_count = jnp.sum(
        jnp.where(jnp.arange(experts, dtype=jnp.int32) == own_expert, global_counts, 0.0)
    )
    factor = 2.0 / jnp.maximum(own_count, 1.0)
    all_tokens, all_hidden = (
        lax.all_gather(slot_tokens, "dp", axis=0, tiled=True),
        lax.all_gather(slot_hidden, "dp", axis=0, tiled=True),
    )
    width_tokens = slot_tokens.shape[1] * tiles // senders
    width_hidden = slot_hidden.shape[1] * tiles // senders
    group_index = lax.axis_index("dp")
    if senders % tiles == 0:
        source_tile = group_index * tiles // senders
        offset_tokens = group_index * width_tokens - source_tile * slot_tokens.shape[1]
        offset_hidden = group_index * width_hidden - source_tile * slot_hidden.shape[1]
        own_tokens = lax.dynamic_slice_in_dim(all_tokens, offset_tokens, width_tokens, 1)
        own_hidden = lax.dynamic_slice_in_dim(all_hidden, offset_hidden, width_hidden, 1)
        joined = jnp.concatenate([own_tokens, own_hidden], axis=1)
        arrived = broadcast(joined, "tile", source_tile)
        column_tokens = arrived[:, :width_tokens]
        column_hidden = arrived[:, width_tokens:]
    else:
        wide_tokens, wide_hidden = (
            lax.all_gather(all_tokens, "tile", axis=1, tiled=True),
            lax.all_gather(all_hidden, "tile", axis=1, tiled=True),
        )
        column_tokens = lax.dynamic_slice_in_dim(
            wide_tokens, group_index * width_tokens, width_tokens, 1
        )
        column_hidden = lax.dynamic_slice_in_dim(
            wide_hidden, group_index * width_hidden, width_hidden, 1
        )
    gram_tokens = contract(all_tokens, column_tokens)
    gram_hidden = contract(all_hidden, column_hidden)
    return ((gram_tokens * factor)[None], (gram_hidden * factor)[None])


def packed_rows(tokens, hidden, routes, live_count, experts, cap):
    token_count, top_count = routes.shape
    flat_routes = routes.reshape(token_count * top_count)
    pair_index = jnp.arange(token_count * top_count, dtype=jnp.int32)
    pair_live = pair_index // top_count < live_count
    expert_ids = jnp.arange(experts, dtype=jnp.int32)
    onehot = ((flat_routes[:, None] == expert_ids[None, :]) & pair_live[:, None]).astype(
        jnp.float32
    )
    earlier = (pair_index[None, :] < pair_index[:, None]).astype(jnp.float32)
    before = jnp.dot(earlier, onehot)
    position = jnp.sum(before * onehot, axis=1).astype(jnp.int32)
    target = jnp.where(pair_live, flat_routes * cap + position, -1)
    placed = (target[None, :] == jnp.arange(experts * cap, dtype=jnp.int32)[:, None]).astype(
        jnp.bfloat16
    )
    by_token = jnp.sum(placed.reshape(experts * cap, token_count, top_count), axis=2)
    send_tokens = jnp.dot(by_token, tokens, preferred_element_type=jnp.float32)
    flat_hidden = hidden.reshape(token_count * top_count, hidden.shape[2])
    send_hidden = jnp.dot(placed, flat_hidden, preferred_element_type=jnp.float32)
    packed = jnp.concatenate(
        [send_tokens.astype(jnp.bfloat16), send_hidden.astype(jnp.bfloat16)], axis=1
    )
    return packed.reshape(experts, cap, packed.shape[1]), jnp.sum(onehot, axis=0)


def exchange(experts, own_ref, count_ref, all_ref, counts_ref, local_sem, send_sem, recv_sem,
             count_send, count_recv):
    d, e, t = lax.axis_index("dp"), lax.axis_index("expert"), lax.axis_index("tile")
    x, c = t // 2, t % 2
    other = 1 - d
    unequal = (x + d) % 2
    own_slot = (1 - unequal) * c + unequal * 2
    along_y = {"dp": other, "expert": e, "tile": t}
    along_x = {"dp": d, "expert": e, "tile": t + 2 - 4 * x}
    sibling = {"dp": d, "expert": e, "tile": t + 1 - 2 * c}
    peers = [{"dp": d, "expert": (e + k) % experts, "tile": t} for k in range(1, experts)]
    far = [{"dp": other, "expert": (e + k) % experts, "tile": t} for k in range(experts)]

    barrier = pltpu.get_barrier_semaphore()
    greeted = peers + far + [along_x, sibling]
    for peer in greeted:
        pl.semaphore_signal(barrier, inc=1, device_id=peer, device_id_type=MESH)
    pl.semaphore_wait(barrier, len(greeted))

    def send(source, slot, group, z, peer, kind, k):
        copy = pltpu.make_async_remote_copy(
            src_ref=source,
            dst_ref=all_ref.at[slot, group, z],
            send_sem=send_sem.at[kind, k],
            recv_sem=recv_sem.at[slot, group, z],
            device_id=peer,
            device_id_type=MESH,
        )
        copy.start()
        return copy

    def arrived(slot, group, z):
        pltpu.make_async_copy(
            all_ref.at[slot, group, z], all_ref.at[slot, group, z], recv_sem.at[slot, group, z]
        ).wait()

    first = [
        send(own_ref.at[(e + k) % experts], own_slot, d, e, peers[k - 1], 0, k)
        for k in range(1, experts)
    ]
    local = pltpu.make_async_copy(own_ref.at[e], all_ref.at[own_slot, d, e], local_sem.at[0])
    local.start()
    zs = [(e + experts - k) % experts for k in range(experts)]

    def source(slot, k):
        return own_ref.at[e] if k == 0 else all_ref.at[slot, d, zs[k]]

    @pl.when(unequal == 0)
    def _():
        started = []

        def relay(k):
            z = zs[k]
            arrived(c, other, z)
            held = all_ref.at[c, other, z]
            if k % 2 == 0:
                started.append(send(held, c, other, z, along_x, 5, k))
            started.append(send(held, c, other, z, sibling, 4, k))
            if k % 2 == 1:
                arrived(2, d, z)
                started.append(send(all_ref.at[2, d, z], c, d, z, along_y, 5, k))

        for k in range(experts):
            if k:
                arrived(c, d, zs[k])
            started.append(send(source(c, k), c, d, zs[k], along_x, 2, k))
            started.append(send(source(c, k), 2, d, zs[k], along_y, 1, k))
            started.append(send(source(c, k), c, d, zs[k], sibling, 3, k))
            if k:
                relay(k - 1)
        relay(experts - 1)
        for k in range(experts):
            arrived(1 - c, d, zs[k])
            arrived(1 - c, other, zs[k])
        for copy in started:
            copy.wait_send()

    @pl.when(unequal == 1)
    def _():
        started = []

        def share(group, k, kind):
            arrived(c, group, zs[k])
            started.append(
                send(all_ref.at[c, group, zs[k]], c, group, zs[k], sibling, kind, k)
            )

        for k in range(experts):
            if k:
                arrived(2, d, zs[k])
            started.append(send(source(2, k), c, d, zs[k], along_y, 1, k))
            if k % 2 == 1:
                started.append(send(source(2, k), 2, d, zs[k], along_x, 2, k))
            if k >= 1:
                share(d, k - 1, 3)
            if k >= 2:
                share(other, k - 2, 4)
        share(d, experts - 1, 3)
        for k in range(max(experts - 2, 0), experts):
            share(other, k, 4)
        for k in range(experts):
            arrived(2, other, zs[k])
            arrived(1 - c, d, zs[k])
            arrived(1 - c, other, zs[k])
        for copy in started:
            copy.wait_send()

    told = []
    for index, peer in enumerate(peers + far):
        copy = pltpu.make_async_remote_copy(
            src_ref=count_ref.at[peer["expert"]],
            dst_ref=counts_ref.at[d, e],
            send_sem=count_send.at[index],
            recv_sem=count_recv.at[d, e],
            device_id=peer,
            device_id_type=MESH,
        )
        copy.start()
        told.append(copy)
    own_count = pltpu.make_async_copy(count_ref.at[e], counts_ref.at[d, e], local_sem.at[1])
    own_count.start()
    for peer in peers + far:
        pltpu.make_async_copy(
            counts_ref.at[peer["dp"], peer["expert"]],
            counts_ref.at[peer["dp"], peer["expert"]],
            count_recv.at[peer["dp"], peer["expert"]],
        ).wait()
    for copy in told + first:
        copy.wait_send()
    own_count.wait()
    local.wait()


def grams(steps_down, width_in, sel_ref, left_ref, columns_ref, counts_ref, in_ref, down_ref):
    step = pl.program_id(0)
    total = jnp.sum(counts_ref[...], axis=0)[0:1, 0:1]
    factor = 2.0 / jnp.maximum(total, 1.0)
    left = left_ref[0]

    def fill(out_ref, start, width):
        for k in range(2):
            for at in range(0, width, width // 2):
                out_ref[0, :, k * width + at : k * width + at + width // 2] = (
                    contract(
                        left, columns_ref[k, :, start + at : start + at + width // 2]
                    )
                    * factor
                )

    @pl.when(step < steps_down)
    def _():
        fill(down_ref, width_in, columns_ref.shape[2] - width_in)

    @pl.when(step >= steps_down)
    def _():
        fill(in_ref, 0, width_in)


def direct(tokens, hidden, routes, lengths, cap):
    experts = lax.axis_size("expert")
    width_in, width_down = tokens.shape[1], hidden.shape[2]
    features = width_in + width_down
    packed, local_counts = packed_rows(tokens, hidden, routes, lengths[0], experts, cap)
    count_tiles = jnp.broadcast_to(local_counts[:, None, None], (experts, 8, 128))
    gathered, counts = pl.pallas_call(
        functools.partial(exchange, experts),
        out_shape=(
            jax.ShapeDtypeStruct((3, 2, experts, cap, features), jnp.bfloat16),
            jax.ShapeDtypeStruct((2, experts, 8, 128), jnp.float32),
        ),
        in_specs=[pl.BlockSpec(memory_space=pltpu.VMEM)] * 2,
        out_specs=[pl.BlockSpec(memory_space=pl.ANY)] * 2,
        scratch_shapes=[
            pltpu.SemaphoreType.DMA((2,)),
            pltpu.SemaphoreType.DMA((6, experts)),
            pltpu.SemaphoreType.DMA((3, 2, experts)),
            pltpu.SemaphoreType.DMA((2 * experts - 1,)),
            pltpu.SemaphoreType.DMA((2, experts)),
        ],
        compiler_params=pltpu.CompilerParams(collective_id=0, has_side_effects=True),
        name="exchange",
    )(packed, count_tiles)
    rows = 2 * experts * cap
    tile, group = lax.axis_index("tile"), lax.axis_index("dp")
    left_slot = jnp.where(tile // 2 == group, tile % 2, 2).astype(jnp.int32).reshape(1)
    steps_in, steps_down = width_in // ROW_BLOCK, width_down // ROW_BLOCK
    steps = steps_in + steps_down
    joined = gathered.reshape(3, rows, features)
    return pl.pallas_call(
        functools.partial(grams, steps_down, width_in),
        out_shape=(
            jax.ShapeDtypeStruct((1, width_in, 2 * width_in), jnp.float32),
            jax.ShapeDtypeStruct((1, width_down, 2 * width_down), jnp.float32),
        ),
        grid_spec=pltpu.PrefetchScalarGridSpec(
            num_scalar_prefetch=1,
            grid=(steps,),
            in_specs=[
                pl.BlockSpec(
                    (1, rows, ROW_BLOCK), lambda i, sel: (sel[0], 0, (i + steps_in) % steps)
                ),
                pl.BlockSpec((2, rows, features), lambda i, sel: (0, 0, 0)),
                pl.BlockSpec((2 * experts, 8, 128), lambda i, sel: (0, 0, 0)),
            ],
            out_specs=(
                pl.BlockSpec(
                    (1, ROW_BLOCK, 2 * width_in),
                    lambda i, sel: (0, jnp.maximum(i - steps_down, 0), 0),
                ),
                pl.BlockSpec(
                    (1, ROW_BLOCK, 2 * width_down),
                    lambda i, sel: (0, jnp.minimum(i, steps_down - 1), 0),
                ),
            ),
        ),
        compiler_params=pltpu.CompilerParams(
            dimension_semantics=("arbitrary",), vmem_limit_bytes=48 * 1024 * 1024
        ),
        name="grams",
    )(left_slot, joined, joined, counts.reshape(2 * experts, 8, 128))


def on_device(tokens, hidden, routes, lengths):
    experts = lax.axis_size("expert")
    senders = lax.axis_size("dp")
    token_count = tokens.shape[0]
    share_size = (5 * token_count + 2 * experts * senders - 1) // (2 * experts * senders)
    cap = share_size * senders
    fits = tokens.shape[1] % ROW_BLOCK == 0 and hidden.shape[2] % ROW_BLOCK == 0
    if senders == 2 and lax.axis_size("tile") == 4 and cap % 8 == 0 and fits:
        return direct(tokens, hidden, routes, lengths, cap)
    return general(tokens, hidden, routes, lengths)


def solution(mesh):
    placed = (
        P(("dp", "expert"), "tile"),
        P(("dp", "expert"), None, "tile"),
        P(("dp", "expert"), None),
        P(("dp", "expert")),
    )
    return jax.shard_map(
        on_device,
        mesh=mesh,
        in_specs=placed,
        out_specs=(P("expert", "tile", "dp"), P("expert", "tile", "dp")),
        check_vma=False,
    )
```

```python
import functools

import jax
import jax.numpy as jnp
from jax import lax
from jax.experimental import pallas as pl
from jax.experimental.pallas import tpu as pltpu
from jax.sharding import PartitionSpec as P

MESH = pl.DeviceIdType.MESH
ROW_BLOCK = 256


def broadcast(value, axis, source):
    kept = jnp.where(lax.axis_index(axis) == source, value, 0).astype(value.dtype)
    return lax.psum(kept, axis)


def contract(left, right):
    return lax.dot_general(
        left, right, (((0,), (0,)), ((), ())), preferred_element_type=jnp.float32
    )


def dispatch_tables(routes, live_count, experts, share_size, senders):
    token_count = routes.shape[0]
    top_count = routes.shape[1]
    flat_routes = routes.reshape(token_count * top_count)
    pair_index = jnp.arange(token_count * top_count, dtype=jnp.int32)
    pair_live = pair_index // top_count < live_count
    expert_ids = jnp.arange(experts, dtype=jnp.int32)
    onehot = ((flat_routes[:, None] == expert_ids[None, :]) & pair_live[:, None]).astype(
        jnp.float32
    )
    before = jnp.cumsum(onehot, axis=0) - onehot
    position = jnp.sum(before * onehot, axis=1).astype(jnp.int32)
    target = (
        position // share_size * (experts * share_size)
        + flat_routes * share_size
        + position % share_size
    )
    slot_total = senders * experts * share_size
    placed = (target[None, :] == jnp.arange(slot_total, dtype=jnp.int32)[:, None]) & pair_live[
        None, :
    ]
    return (placed.astype(jnp.float32), jnp.sum(onehot, axis=0))


def general(tokens, hidden, routes, lengths):
    experts = lax.axis_size("expert")
    senders = lax.axis_size("dp")
    tiles = lax.axis_size("tile")
    token_count = tokens.shape[0]
    top_count = routes.shape[1]
    share_size = (5 * token_count + 2 * experts * senders - 1) // (2 * experts * senders)
    placed, local_counts = dispatch_tables(routes, lengths[0], experts, share_size, senders)
    slot_total = placed.shape[0]
    by_token = jnp.sum(placed.reshape(slot_total, token_count, top_count), axis=2).astype(
        jnp.bfloat16
    )
    send_tokens = jnp.dot(by_token, tokens, preferred_element_type=jnp.float32).astype(jnp.bfloat16)
    flat_hidden = hidden.reshape(token_count * top_count, hidden.shape[2])
    send_hidden = jnp.dot(
        placed.astype(jnp.bfloat16), flat_hidden, preferred_element_type=jnp.float32
    ).astype(jnp.bfloat16)
    slot_tokens, slot_hidden = (
        lax.all_to_all(send_tokens, ("dp", "expert"), split_axis=0, concat_axis=0, tiled=True),
        lax.all_to_all(send_hidden, ("dp", "expert"), split_axis=0, concat_axis=0, tiled=True),
    )
    global_counts = lax.psum(local_counts, ("dp", "expert"))
    own_expert = lax.axis_index("expert")
    own_count = jnp.sum(
        jnp.where(jnp.arange(experts, dtype=jnp.int32) == own_expert, global_counts, 0.0)
    )
    factor = 2.0 / jnp.maximum(own_count, 1.0)
    all_tokens, all_hidden = (
        lax.all_gather(slot_tokens, "dp", axis=0, tiled=True),
        lax.all_gather(slot_hidden, "dp", axis=0, tiled=True),
    )
    width_tokens = slot_tokens.shape[1] * tiles // senders
    width_hidden = slot_hidden.shape[1] * tiles // senders
    group_index = lax.axis_index("dp")
    if senders % tiles == 0:
        source_tile = group_index * tiles // senders
        offset_tokens = group_index * width_tokens - source_tile * slot_tokens.shape[1]
        offset_hidden = group_index * width_hidden - source_tile * slot_hidden.shape[1]
        own_tokens = lax.dynamic_slice_in_dim(all_tokens, offset_tokens, width_tokens, 1)
        own_hidden = lax.dynamic_slice_in_dim(all_hidden, offset_hidden, width_hidden, 1)
        joined = jnp.concatenate([own_tokens, own_hidden], axis=1)
        arrived = broadcast(joined, "tile", source_tile)
        column_tokens = arrived[:, :width_tokens]
        column_hidden = arrived[:, width_tokens:]
    else:
        wide_tokens, wide_hidden = (
            lax.all_gather(all_tokens, "tile", axis=1, tiled=True),
            lax.all_gather(all_hidden, "tile", axis=1, tiled=True),
        )
        column_tokens = lax.dynamic_slice_in_dim(
            wide_tokens, group_index * width_tokens, width_tokens, 1
        )
        column_hidden = lax.dynamic_slice_in_dim(
            wide_hidden, group_index * width_hidden, width_hidden, 1
        )
    gram_tokens = contract(all_tokens, column_tokens)
    gram_hidden = contract(all_hidden, column_hidden)
    return ((gram_tokens * factor)[None], (gram_hidden * factor)[None])


def pack(experts, cap, live_ref, routes_ref, tokens_ref, hidden_ref, packed_ref, count_ref):
    token_count, width_in = tokens_ref.shape
    routes = routes_ref[...]
    row = lax.broadcasted_iota(jnp.int32, (1, token_count), 1)
    live = row < live_ref[0]
    first, second = routes[0:1], routes[1:2]
    expert_ids = lax.broadcasted_iota(jnp.int32, (experts, token_count), 0)
    hits = jnp.where(((first == expert_ids) | (second == expert_ids)) & live, 1.0, 0.0)
    earlier = jnp.where(
        lax.broadcasted_iota(jnp.int32, (token_count, token_count), 0)
        < lax.broadcasted_iota(jnp.int32, (token_count, token_count), 1),
        1.0,
        0.0,
    )
    before = jnp.dot(
        hits.astype(jnp.bfloat16), earlier.astype(jnp.bfloat16), preferred_element_type=jnp.float32
    )
    slot = lax.broadcasted_iota(jnp.int32, (cap, token_count), 0).astype(jnp.float32)
    by_first, by_second = [], []
    for expert in range(experts):
        hit = hits[expert : expert + 1]
        placed = jnp.where(slot == before[expert : expert + 1], hit, 0.0)
        by_first.append(jnp.where(first == expert, placed, 0.0))
        by_second.append(jnp.where(second == expert, placed, 0.0))
        total = jnp.sum(hit, axis=1, keepdims=True)
        count_ref[expert] = jnp.broadcast_to(total, count_ref.shape[1:])
    by_first = jnp.concatenate(by_first, axis=0)
    by_second = jnp.concatenate(by_second, axis=0)
    by_token = (by_first + by_second).astype(jnp.bfloat16)
    by_first, by_second = by_first.astype(jnp.bfloat16), by_second.astype(jnp.bfloat16)

    def put(rows, start):
        for expert in range(experts):
            packed_ref[expert, :, start : start + rows.shape[1]] = rows[
                expert * cap : (expert + 1) * cap
            ].astype(jnp.bfloat16)

    put(jnp.dot(by_token, tokens_ref[...], preferred_element_type=jnp.float32), 0)
    put(
        jnp.dot(by_first, hidden_ref[:, 0, :], preferred_element_type=jnp.float32)
        + jnp.dot(by_second, hidden_ref[:, 1, :], preferred_element_type=jnp.float32),
        width_in,
    )


def exchange(experts, own_ref, count_ref, all_ref, counts_ref, local_sem, send_sem, recv_sem,
             count_send, count_recv):
    d, e, t = lax.axis_index("dp"), lax.axis_index("expert"), lax.axis_index("tile")
    x, c = t // 2, t % 2
    other = 1 - d
    unequal = (x + d) % 2
    own_slot = (1 - unequal) * c + unequal * 2
    along_y = {"dp": other, "expert": e, "tile": t}
    along_x = {"dp": d, "expert": e, "tile": t + 2 - 4 * x}
    sibling = {"dp": d, "expert": e, "tile": t + 1 - 2 * c}
    peers = [{"dp": d, "expert": (e + k) % experts, "tile": t} for k in range(1, experts)]
    far = [{"dp": other, "expert": (e + k) % experts, "tile": t} for k in range(experts)]

    barrier = pltpu.get_barrier_semaphore()
    greeted = peers + far + [along_x, sibling]
    for peer in greeted:
        pl.semaphore_signal(barrier, inc=1, device_id=peer, device_id_type=MESH)
    pl.semaphore_wait(barrier, len(greeted))

    def send(source, slot, group, z, peer, kind, k):
        copy = pltpu.make_async_remote_copy(
            src_ref=source,
            dst_ref=all_ref.at[slot, group, z],
            send_sem=send_sem.at[kind, k],
            recv_sem=recv_sem.at[slot, group, z],
            device_id=peer,
            device_id_type=MESH,
        )
        copy.start()
        return copy

    def arrived(slot, group, z):
        pltpu.make_async_copy(
            all_ref.at[slot, group, z], all_ref.at[slot, group, z], recv_sem.at[slot, group, z]
        ).wait()

    low = e // 2
    zs = [e, 1 - e + 4 * low, 2 - low, 3 - 3 * low]
    middle = (e + low) % 2

    first = [
        pltpu.make_async_remote_copy(
            src_ref=own_ref.at[zs[k]],
            dst_ref=all_ref.at[own_slot, d, e],
            send_sem=send_sem.at[0, k],
            recv_sem=recv_sem.at[own_slot, d, e],
            device_id={"dp": d, "expert": zs[k], "tile": t},
            device_id_type=MESH,
        )
        for k in range(1, experts)
    ]
    first[0].start()

    @pl.when(middle == 1)
    def _():
        first[1].start()

    local = pltpu.make_async_copy(own_ref.at[e], all_ref.at[own_slot, d, e], local_sem.at[0])
    local.start()

    def second_sends():
        first[0].wait_send()

        @pl.when(middle == 0)
        def _():
            first[1].start()

        @pl.when(middle == 1)
        def _():
            first[1].wait_send()
            first[2].start()

    def third_sends():
        @pl.when(middle == 0)
        def _():
            first[1].wait_send()
            first[2].start()

    def source(slot, k):
        return own_ref.at[e] if k == 0 else all_ref.at[slot, d, zs[k]]

    @pl.when(unequal == 0)
    def _():
        started = []

        def relay(k):
            z = zs[k]
            arrived(c, other, z)
            held = all_ref.at[c, other, z]
            if k % 2 == 0:
                started.append(send(held, c, other, z, along_x, 5, k))
            started.append(send(held, c, other, z, sibling, 4, k))
            if k % 2 == 1:
                arrived(2, d, z)
                started.append(send(all_ref.at[2, d, z], c, d, z, along_y, 5, k))

        for k in range(experts):
            if k:
                arrived(c, d, zs[k])
            started.append(send(source(c, k), c, d, zs[k], along_x, 2, k))
            started.append(send(source(c, k), 2, d, zs[k], along_y, 1, k))
            started.append(send(source(c, k), c, d, zs[k], sibling, 3, k))
            if k == 0:
                second_sends()
            relay(k)
            if k == 1:
                third_sends()
        for k in range(experts):
            arrived(1 - c, d, zs[k])
            arrived(1 - c, other, zs[k])
        for copy in started:
            copy.wait_send()

    @pl.when(unequal == 1)
    def _():
        started = []

        def share(group, k, kind):
            arrived(c, group, zs[k])
            started.append(
                send(all_ref.at[c, group, zs[k]], c, group, zs[k], sibling, kind, k)
            )

        for k in range(experts):
            if k:
                arrived(2, d, zs[k])
            started.append(send(source(2, k), c, d, zs[k], along_y, 1, k))
            if k % 2 == 1:
                started.append(send(source(2, k), 2, d, zs[k], along_x, 2, k))
            if k == 0:
                second_sends()
            if k >= 1:
                share(other, k - 1, 4)
            if k == 1:
                third_sends()
            share(d, k, 3)
        share(other, experts - 1, 4)
        for k in range(experts):
            arrived(2, other, zs[k])
            arrived(1 - c, d, zs[k])
            arrived(1 - c, other, zs[k])
        for copy in started:
            copy.wait_send()

    told = []
    for index, peer in enumerate(peers + far):
        copy = pltpu.make_async_remote_copy(
            src_ref=count_ref.at[peer["expert"]],
            dst_ref=counts_ref.at[d, e],
            send_sem=count_send.at[index],
            recv_sem=count_recv.at[d, e],
            device_id=peer,
            device_id_type=MESH,
        )
        copy.start()
        told.append(copy)
    own_count = pltpu.make_async_copy(count_ref.at[e], counts_ref.at[d, e], local_sem.at[1])
    own_count.start()
    for peer in peers + far:
        pltpu.make_async_copy(
            counts_ref.at[peer["dp"], peer["expert"]],
            counts_ref.at[peer["dp"], peer["expert"]],
            count_recv.at[peer["dp"], peer["expert"]],
        ).wait()
    for copy in told + first[2:]:
        copy.wait_send()
    own_count.wait()
    local.wait()


def grams(steps_down, width_in, sel_ref, left_ref, columns_ref, counts_ref, in_ref, down_ref):
    step = pl.program_id(0)
    total = jnp.sum(counts_ref[...], axis=0)[0:1, 0:1]
    factor = 2.0 / jnp.maximum(total, 1.0)
    left = left_ref[0]

    def fill(out_ref, start, width):
        for k in range(2):
            for at in range(0, width, width // 2):
                out_ref[0, :, k * width + at : k * width + at + width // 2] = (
                    contract(
                        left, columns_ref[k, :, start + at : start + at + width // 2]
                    )
                    * factor
                )

    @pl.when(step < steps_down)
    def _():
        fill(down_ref, width_in, columns_ref.shape[2] - width_in)

    @pl.when(step >= steps_down)
    def _():
        fill(in_ref, 0, width_in)


def direct(tokens, hidden, routes, lengths, cap):
    experts = lax.axis_size("expert")
    width_in, width_down = tokens.shape[1], hidden.shape[2]
    features = width_in + width_down
    vmem = pl.BlockSpec(memory_space=pltpu.VMEM)
    packed, count_tiles = pl.pallas_call(
        functools.partial(pack, experts, cap),
        out_shape=(
            jax.ShapeDtypeStruct((experts, cap, features), jnp.bfloat16),
            jax.ShapeDtypeStruct((experts, 8, 128), jnp.float32),
        ),
        in_specs=[pl.BlockSpec(memory_space=pltpu.SMEM), vmem, vmem, vmem],
        out_specs=[vmem, vmem],
        name="pack",
    )(lengths, routes.T, tokens, hidden)
    gathered, counts = pl.pallas_call(
        functools.partial(exchange, experts),
        out_shape=(
            jax.ShapeDtypeStruct((3, 2, experts, cap, features), jnp.bfloat16),
            jax.ShapeDtypeStruct((2, experts, 8, 128), jnp.float32),
        ),
        in_specs=[vmem, vmem],
        out_specs=[pl.BlockSpec(memory_space=pl.ANY)] * 2,
        scratch_shapes=[
            pltpu.SemaphoreType.DMA((2,)),
            pltpu.SemaphoreType.DMA((6, experts)),
            pltpu.SemaphoreType.DMA((3, 2, experts)),
            pltpu.SemaphoreType.DMA((2 * experts - 1,)),
            pltpu.SemaphoreType.DMA((2, experts)),
        ],
        compiler_params=pltpu.CompilerParams(collective_id=0, has_side_effects=True),
        name="exchange",
    )(packed, count_tiles)
    rows = 2 * experts * cap
    tile, group = lax.axis_index("tile"), lax.axis_index("dp")
    left_slot = jnp.where(tile // 2 == group, tile % 2, 2).astype(jnp.int32).reshape(1)
    steps_in, steps_down = width_in // ROW_BLOCK, width_down // ROW_BLOCK
    steps = steps_in + steps_down
    joined = gathered.reshape(3, rows, features)
    return pl.pallas_call(
        functools.partial(grams, steps_down, width_in),
        out_shape=(
            jax.ShapeDtypeStruct((1, width_in, 2 * width_in), jnp.float32),
            jax.ShapeDtypeStruct((1, width_down, 2 * width_down), jnp.float32),
        ),
        grid_spec=pltpu.PrefetchScalarGridSpec(
            num_scalar_prefetch=1,
            grid=(steps,),
            in_specs=[
                pl.BlockSpec(
                    (1, rows, ROW_BLOCK), lambda i, sel: (sel[0], 0, (i + steps_in) % steps)
                ),
                pl.BlockSpec((2, rows, features), lambda i, sel: (0, 0, 0)),
                pl.BlockSpec((2 * experts, 8, 128), lambda i, sel: (0, 0, 0)),
            ],
            out_specs=(
                pl.BlockSpec(
                    (1, ROW_BLOCK, 2 * width_in),
                    lambda i, sel: (0, jnp.maximum(i - steps_down, 0), 0),
                ),
                pl.BlockSpec(
                    (1, ROW_BLOCK, 2 * width_down),
                    lambda i, sel: (0, jnp.minimum(i, steps_down - 1), 0),
                ),
            ),
        ),
        compiler_params=pltpu.CompilerParams(
            dimension_semantics=("arbitrary",), vmem_limit_bytes=66_000_000
        ),
        name="grams",
    )(left_slot, joined, joined, counts.reshape(2 * experts, 8, 128))


def on_device(tokens, hidden, routes, lengths):
    experts = lax.axis_size("expert")
    senders = lax.axis_size("dp")
    token_count = tokens.shape[0]
    share_size = (5 * token_count + 2 * experts * senders - 1) // (2 * experts * senders)
    cap = share_size * senders
    fits = tokens.shape[1] % ROW_BLOCK == 0 and hidden.shape[2] % ROW_BLOCK == 0
    square = senders == 2 and experts == 4 and lax.axis_size("tile") == 4 and routes.shape[1] == 2
    if square and cap % 8 == 0 and fits:
        return direct(tokens, hidden, routes, lengths, cap)
    return general(tokens, hidden, routes, lengths)


def solution(mesh):
    placed = (
        P(("dp", "expert"), "tile"),
        P(("dp", "expert"), None, "tile"),
        P(("dp", "expert"), None),
        P(("dp", "expert")),
    )
    return jax.shard_map(
        on_device,
        mesh=mesh,
        in_specs=placed,
        out_specs=(P("expert", "tile", "dp"), P("expert", "tile", "dp")),
        check_vma=False,
    )
```

```python
import functools

import jax
import jax.numpy as jnp
from jax import lax
from jax.experimental import pallas as pl
from jax.experimental.pallas import tpu as pltpu
from jax.sharding import PartitionSpec as P

MESH = pl.DeviceIdType.MESH
ROW_BLOCK = 256
PIECES = 2


def broadcast(value, axis, source):
    kept = jnp.where(lax.axis_index(axis) == source, value, 0).astype(value.dtype)
    return lax.psum(kept, axis)


def contract(left, right):
    return lax.dot_general(
        left, right, (((0,), (0,)), ((), ())), preferred_element_type=jnp.float32
    )


def dispatch_tables(routes, live_count, experts, share_size, senders):
    token_count = routes.shape[0]
    top_count = routes.shape[1]
    flat_routes = routes.reshape(token_count * top_count)
    pair_index = jnp.arange(token_count * top_count, dtype=jnp.int32)
    pair_live = pair_index // top_count < live_count
    expert_ids = jnp.arange(experts, dtype=jnp.int32)
    onehot = ((flat_routes[:, None] == expert_ids[None, :]) & pair_live[:, None]).astype(
        jnp.float32
    )
    before = jnp.cumsum(onehot, axis=0) - onehot
    position = jnp.sum(before * onehot, axis=1).astype(jnp.int32)
    target = (
        position // share_size * (experts * share_size)
        + flat_routes * share_size
        + position % share_size
    )
    slot_total = senders * experts * share_size
    placed = (target[None, :] == jnp.arange(slot_total, dtype=jnp.int32)[:, None]) & pair_live[
        None, :
    ]
    return (placed.astype(jnp.float32), jnp.sum(onehot, axis=0))


def general(tokens, hidden, routes, lengths):
    experts = lax.axis_size("expert")
    senders = lax.axis_size("dp")
    tiles = lax.axis_size("tile")
    token_count = tokens.shape[0]
    top_count = routes.shape[1]
    share_size = (5 * token_count + 2 * experts * senders - 1) // (2 * experts * senders)
    placed, local_counts = dispatch_tables(routes, lengths[0], experts, share_size, senders)
    slot_total = placed.shape[0]
    by_token = jnp.sum(placed.reshape(slot_total, token_count, top_count), axis=2).astype(
        jnp.bfloat16
    )
    send_tokens = jnp.dot(by_token, tokens, preferred_element_type=jnp.float32).astype(jnp.bfloat16)
    flat_hidden = hidden.reshape(token_count * top_count, hidden.shape[2])
    send_hidden = jnp.dot(
        placed.astype(jnp.bfloat16), flat_hidden, preferred_element_type=jnp.float32
    ).astype(jnp.bfloat16)
    slot_tokens, slot_hidden = (
        lax.all_to_all(send_tokens, ("dp", "expert"), split_axis=0, concat_axis=0, tiled=True),
        lax.all_to_all(send_hidden, ("dp", "expert"), split_axis=0, concat_axis=0, tiled=True),
    )
    global_counts = lax.psum(local_counts, ("dp", "expert"))
    own_expert = lax.axis_index("expert")
    own_count = jnp.sum(
        jnp.where(jnp.arange(experts, dtype=jnp.int32) == own_expert, global_counts, 0.0)
    )
    factor = 2.0 / jnp.maximum(own_count, 1.0)
    all_tokens, all_hidden = (
        lax.all_gather(slot_tokens, "dp", axis=0, tiled=True),
        lax.all_gather(slot_hidden, "dp", axis=0, tiled=True),
    )
    width_tokens = slot_tokens.shape[1] * tiles // senders
    width_hidden = slot_hidden.shape[1] * tiles // senders
    group_index = lax.axis_index("dp")
    if senders % tiles == 0:
        source_tile = group_index * tiles // senders
        offset_tokens = group_index * width_tokens - source_tile * slot_tokens.shape[1]
        offset_hidden = group_index * width_hidden - source_tile * slot_hidden.shape[1]
        own_tokens = lax.dynamic_slice_in_dim(all_tokens, offset_tokens, width_tokens, 1)
        own_hidden = lax.dynamic_slice_in_dim(all_hidden, offset_hidden, width_hidden, 1)
        joined = jnp.concatenate([own_tokens, own_hidden], axis=1)
        arrived = broadcast(joined, "tile", source_tile)
        column_tokens = arrived[:, :width_tokens]
        column_hidden = arrived[:, width_tokens:]
    else:
        wide_tokens, wide_hidden = (
            lax.all_gather(all_tokens, "tile", axis=1, tiled=True),
            lax.all_gather(all_hidden, "tile", axis=1, tiled=True),
        )
        column_tokens = lax.dynamic_slice_in_dim(
            wide_tokens, group_index * width_tokens, width_tokens, 1
        )
        column_hidden = lax.dynamic_slice_in_dim(
            wide_hidden, group_index * width_hidden, width_hidden, 1
        )
    gram_tokens = contract(all_tokens, column_tokens)
    gram_hidden = contract(all_hidden, column_hidden)
    return ((gram_tokens * factor)[None], (gram_hidden * factor)[None])


def pack(experts, cap, live_ref, routes_ref, tokens_ref, hidden_ref, packed_ref, count_ref):
    token_count, width_in = tokens_ref.shape
    routes = routes_ref[...]
    row = lax.broadcasted_iota(jnp.int32, (1, token_count), 1)
    live = row < live_ref[0]
    first, second = routes[0:1], routes[1:2]
    expert_ids = lax.broadcasted_iota(jnp.int32, (experts, token_count), 0)
    hits = jnp.where(((first == expert_ids) | (second == expert_ids)) & live, 1.0, 0.0)
    earlier = jnp.where(
        lax.broadcasted_iota(jnp.int32, (token_count, token_count), 0)
        < lax.broadcasted_iota(jnp.int32, (token_count, token_count), 1),
        1.0,
        0.0,
    )
    before = jnp.dot(
        hits.astype(jnp.bfloat16), earlier.astype(jnp.bfloat16), preferred_element_type=jnp.float32
    )
    slot = lax.broadcasted_iota(jnp.int32, (cap, token_count), 0).astype(jnp.float32)
    by_first, by_second = [], []
    for expert in range(experts):
        hit = hits[expert : expert + 1]
        placed = jnp.where(slot == before[expert : expert + 1], hit, 0.0)
        by_first.append(jnp.where(first == expert, placed, 0.0))
        by_second.append(jnp.where(second == expert, placed, 0.0))
        total = jnp.sum(hit, axis=1, keepdims=True)
        count_ref[expert] = jnp.broadcast_to(total, count_ref.shape[1:])
    by_first = jnp.concatenate(by_first, axis=0)
    by_second = jnp.concatenate(by_second, axis=0)
    by_token = (by_first + by_second).astype(jnp.bfloat16)
    by_first, by_second = by_first.astype(jnp.bfloat16), by_second.astype(jnp.bfloat16)

    def put(rows, start):
        for expert in range(experts):
            packed_ref[expert, :, start : start + rows.shape[1]] = rows[
                expert * cap : (expert + 1) * cap
            ].astype(jnp.bfloat16)

    put(jnp.dot(by_token, tokens_ref[...], preferred_element_type=jnp.float32), 0)
    put(
        jnp.dot(by_first, hidden_ref[:, 0, :], preferred_element_type=jnp.float32)
        + jnp.dot(by_second, hidden_ref[:, 1, :], preferred_element_type=jnp.float32),
        width_in,
    )


def exchange(experts, own_ref, count_ref, all_ref, counts_ref, local_sem, send_sem, recv_sem,
             count_send, count_recv):
    d, e, t = lax.axis_index("dp"), lax.axis_index("expert"), lax.axis_index("tile")
    x, c = t // 2, t % 2
    other = 1 - d
    unequal = (x + d) % 2
    own_slot = (1 - unequal) * c + unequal * 2
    along_y = {"dp": other, "expert": e, "tile": t}
    along_x = {"dp": d, "expert": e, "tile": t + 2 - 4 * x}
    sibling = {"dp": d, "expert": e, "tile": t + 1 - 2 * c}
    peers = [{"dp": d, "expert": (e + k) % experts, "tile": t} for k in range(1, experts)]
    far = [{"dp": other, "expert": (e + k) % experts, "tile": t} for k in range(experts)]

    barrier = pltpu.get_barrier_semaphore()
    greeted = peers + far + [along_x, sibling]
    for peer in greeted:
        pl.semaphore_signal(barrier, inc=1, device_id=peer, device_id_type=MESH)
    pl.semaphore_wait(barrier, len(greeted))

    width = all_ref.shape[4] // PIECES
    spans = [pl.ds(piece * width, width) for piece in range(PIECES)]

    def send(source, slot, group, z, peer, kind, k, piece):
        copy = pltpu.make_async_remote_copy(
            src_ref=source.at[:, spans[piece]],
            dst_ref=all_ref.at[slot, group, z, :, spans[piece]],
            send_sem=send_sem.at[kind, k, piece],
            recv_sem=recv_sem.at[slot, group, z, piece],
            device_id=peer,
            device_id_type=MESH,
        )
        copy.start()
        return copy

    def arrived(slot, group, z, piece):
        here = all_ref.at[slot, group, z, :, spans[piece]]
        pltpu.make_async_copy(here, here, recv_sem.at[slot, group, z, piece]).wait()

    low = e // 2
    zs = [e, 1 - e + 4 * low, 2 - low, 3 - 3 * low]
    middle = (e + low) % 2

    first = [
        [
            pltpu.make_async_remote_copy(
                src_ref=own_ref.at[zs[k], :, span],
                dst_ref=all_ref.at[own_slot, d, e, :, span],
                send_sem=send_sem.at[0, k, piece],
                recv_sem=recv_sem.at[own_slot, d, e, piece],
                device_id={"dp": d, "expert": zs[k], "tile": t},
                device_id_type=MESH,
            )
            for piece, span in enumerate(spans)
        ]
        for k in range(1, experts)
    ]

    def start(copies):
        for copy in copies:
            copy.start()

    def left(copies):
        for copy in copies:
            copy.wait_send()

    start(first[0])

    @pl.when(middle == 1)
    def _():
        start(first[1])

    local = pltpu.make_async_copy(own_ref.at[e], all_ref.at[own_slot, d, e], local_sem.at[0])
    local.start()

    def second_sends():
        left(first[0])

        @pl.when(middle == 0)
        def _():
            start(first[1])

        @pl.when(middle == 1)
        def _():
            left(first[1])
            start(first[2])

    def third_sends():
        @pl.when(middle == 0)
        def _():
            left(first[1])
            start(first[2])

    def source(slot, k):
        return own_ref.at[e] if k == 0 else all_ref.at[slot, d, zs[k]]

    pieces = [(k, piece) for k in range(experts) for piece in range(PIECES)]

    @pl.when(unequal == 0)
    def _():
        started = []

        def relay(k, piece):
            z = zs[k]
            arrived(c, other, z, piece)
            held = all_ref.at[c, other, z]
            if k % 2 == 0:
                started.append(send(held, c, other, z, along_x, 5, k, piece))
            started.append(send(held, c, other, z, sibling, 4, k, piece))
            if k % 2 == 1:
                arrived(2, d, z, piece)
                started.append(send(all_ref.at[2, d, z], c, d, z, along_y, 5, k, piece))

        for k in range(experts):
            for piece in range(PIECES):
                if k:
                    arrived(c, d, zs[k], piece)
                started.append(send(source(c, k), c, d, zs[k], along_x, 2, k, piece))
                started.append(send(source(c, k), 2, d, zs[k], along_y, 1, k, piece))
                started.append(send(source(c, k), c, d, zs[k], sibling, 3, k, piece))
            if k == 0:
                second_sends()
            for piece in range(PIECES):
                relay(k, piece)
            if k == 1:
                third_sends()
        for k, piece in pieces:
            arrived(1 - c, d, zs[k], piece)
            arrived(1 - c, other, zs[k], piece)
        left(started)

    @pl.when(unequal == 1)
    def _():
        started = []

        def share(group, k, kind, piece):
            arrived(c, group, zs[k], piece)
            held = all_ref.at[c, group, zs[k]]
            started.append(send(held, c, group, zs[k], sibling, kind, k, piece))

        for k in range(experts):
            for piece in range(PIECES):
                if k:
                    arrived(2, d, zs[k], piece)
                started.append(send(source(2, k), c, d, zs[k], along_y, 1, k, piece))
                if k % 2 == 1:
                    started.append(send(source(2, k), 2, d, zs[k], along_x, 2, k, piece))
            if k == 0:
                second_sends()
            if k == 1:
                third_sends()
        for k, piece in pieces:
            share(d, k, 3, piece)
            share(other, k, 4, piece)
        for k, piece in pieces:
            arrived(2, other, zs[k], piece)
            arrived(1 - c, d, zs[k], piece)
            arrived(1 - c, other, zs[k], piece)
        left(started)

    told = []
    for index, peer in enumerate(peers + far):
        copy = pltpu.make_async_remote_copy(
            src_ref=count_ref.at[peer["expert"]],
            dst_ref=counts_ref.at[d, e],
            send_sem=count_send.at[index],
            recv_sem=count_recv.at[d, e],
            device_id=peer,
            device_id_type=MESH,
        )
        copy.start()
        told.append(copy)
    own_count = pltpu.make_async_copy(count_ref.at[e], counts_ref.at[d, e], local_sem.at[1])
    own_count.start()
    for peer in peers + far:
        pltpu.make_async_copy(
            counts_ref.at[peer["dp"], peer["expert"]],
            counts_ref.at[peer["dp"], peer["expert"]],
            count_recv.at[peer["dp"], peer["expert"]],
        ).wait()
    left(told + first[2])
    own_count.wait()
    local.wait()


def grams(steps_down, width_in, sel_ref, left_ref, columns_ref, counts_ref, in_ref, down_ref):
    step = pl.program_id(0)
    total = jnp.sum(counts_ref[...], axis=0)[0:1, 0:1]
    factor = 2.0 / jnp.maximum(total, 1.0)
    left = left_ref[0]

    def fill(out_ref, start, width):
        for k in range(2):
            for at in range(0, width, width // 2):
                out_ref[0, :, k * width + at : k * width + at + width // 2] = (
                    contract(
                        left, columns_ref[k, :, start + at : start + at + width // 2]
                    )
                    * factor
                )

    @pl.when(step < steps_down)
    def _():
        fill(down_ref, width_in, columns_ref.shape[2] - width_in)

    @pl.when(step >= steps_down)
    def _():
        fill(in_ref, 0, width_in)


def direct(tokens, hidden, routes, lengths, cap):
    experts = lax.axis_size("expert")
    width_in, width_down = tokens.shape[1], hidden.shape[2]
    features = width_in + width_down
    vmem = pl.BlockSpec(memory_space=pltpu.VMEM)
    packed, count_tiles = pl.pallas_call(
        functools.partial(pack, experts, cap),
        out_shape=(
            jax.ShapeDtypeStruct((experts, cap, features), jnp.bfloat16),
            jax.ShapeDtypeStruct((experts, 8, 128), jnp.float32),
        ),
        in_specs=[pl.BlockSpec(memory_space=pltpu.SMEM), vmem, vmem, vmem],
        out_specs=[vmem, vmem],
        name="pack",
    )(lengths, routes.T, tokens, hidden)
    gathered, counts = pl.pallas_call(
        functools.partial(exchange, experts),
        out_shape=(
            jax.ShapeDtypeStruct((3, 2, experts, cap, features), jnp.bfloat16),
            jax.ShapeDtypeStruct((2, experts, 8, 128), jnp.float32),
        ),
        in_specs=[vmem, vmem],
        out_specs=[pl.BlockSpec(memory_space=pl.ANY)] * 2,
        scratch_shapes=[
            pltpu.SemaphoreType.DMA((2,)),
            pltpu.SemaphoreType.DMA((6, experts, PIECES)),
            pltpu.SemaphoreType.DMA((3, 2, experts, PIECES)),
            pltpu.SemaphoreType.DMA((2 * experts - 1,)),
            pltpu.SemaphoreType.DMA((2, experts)),
        ],
        compiler_params=pltpu.CompilerParams(collective_id=0, has_side_effects=True),
        name="exchange",
    )(packed, count_tiles)
    rows = 2 * experts * cap
    tile, group = lax.axis_index("tile"), lax.axis_index("dp")
    left_slot = jnp.where(tile // 2 == group, tile % 2, 2).astype(jnp.int32).reshape(1)
    steps_in, steps_down = width_in // ROW_BLOCK, width_down // ROW_BLOCK
    steps = steps_in + steps_down
    joined = gathered.reshape(3, rows, features)
    return pl.pallas_call(
        functools.partial(grams, steps_down, width_in),
        out_shape=(
            jax.ShapeDtypeStruct((1, width_in, 2 * width_in), jnp.float32),
            jax.ShapeDtypeStruct((1, width_down, 2 * width_down), jnp.float32),
        ),
        grid_spec=pltpu.PrefetchScalarGridSpec(
            num_scalar_prefetch=1,
            grid=(steps,),
            in_specs=[
                pl.BlockSpec(
                    (1, rows, ROW_BLOCK), lambda i, sel: (sel[0], 0, (i + steps_in) % steps)
                ),
                pl.BlockSpec((2, rows, features), lambda i, sel: (0, 0, 0)),
                pl.BlockSpec((2 * experts, 8, 128), lambda i, sel: (0, 0, 0)),
            ],
            out_specs=(
                pl.BlockSpec(
                    (1, ROW_BLOCK, 2 * width_in),
                    lambda i, sel: (0, jnp.maximum(i - steps_down, 0), 0),
                ),
                pl.BlockSpec(
                    (1, ROW_BLOCK, 2 * width_down),
                    lambda i, sel: (0, jnp.minimum(i, steps_down - 1), 0),
                ),
            ),
        ),
        compiler_params=pltpu.CompilerParams(
            dimension_semantics=("arbitrary",), vmem_limit_bytes=66_000_000
        ),
        name="grams",
    )(left_slot, joined, joined, counts.reshape(2 * experts, 8, 128))


def on_device(tokens, hidden, routes, lengths):
    experts = lax.axis_size("expert")
    senders = lax.axis_size("dp")
    token_count = tokens.shape[0]
    share_size = (5 * token_count + 2 * experts * senders - 1) // (2 * experts * senders)
    cap = share_size * senders
    fits = tokens.shape[1] % ROW_BLOCK == 0 and hidden.shape[2] % ROW_BLOCK == 0
    square = senders == 2 and experts == 4 and lax.axis_size("tile") == 4 and routes.shape[1] == 2
    if square and cap % 8 == 0 and fits:
        return direct(tokens, hidden, routes, lengths, cap)
    return general(tokens, hidden, routes, lengths)


def solution(mesh):
    placed = (
        P(("dp", "expert"), "tile"),
        P(("dp", "expert"), None, "tile"),
        P(("dp", "expert"), None),
        P(("dp", "expert")),
    )
    return jax.shard_map(
        on_device,
        mesh=mesh,
        in_specs=placed,
        out_specs=(P("expert", "tile", "dp"), P("expert", "tile", "dp")),
        check_vma=False,
    )
```
